32 devices in a mesh: group: 4 (over y, x), dom: 8 (over z, core).
Axes of the slice: x: 2, y: 2, z: 4, core: 2. Of those that a mesh axis runs over, the one named last changes fastest.
Arguments:
- cotangent: float32 [32, 8, 4096], P(('group', 'dom')), may hold values from -6 to 6
- volumes: float32 [32, 4096], P(('group', 'dom')), may hold values from 0.5 to 2
- ov_target: int32 [32, 7, 4096], P(('group', 'dom')), may hold values from 0 to 4095
- ov_source: int32 [32, 7, 4096], P(('group', 'dom')), may hold values from 0 to 4096, as said below
- volume_moment: float32 [32, 7, 4096], P(('group', 'dom')), may hold values from 0.05 to 1
- first_moment: float32 [32, 3, 7, 4096], P(('group', 'dom')), may hold values from -2 to 2
- grad_weight: float32 [32, 3, 12, 4096], P(('group', 'dom')), may hold values from -2 to 2
- face_nbr: int32 [32, 12, 4096], P(('group', 'dom')), may hold values from 0 to 4351, as said below
- send_map: int32 [32, 2, 128], P(('group', 'dom')), may hold values from 0 to 4095, as said below
Outputs:
- bar_source: float32 [32, 8, 4096], P(('group', 'dom'))
The draws below stay inside these ranges and needn't reach their ends.
Inputs may be any that keep to these rules, and one draw needn't show every extreme that they name: `ov_source`: entry [j, o, k] is the source cell on partition j of slot k that the holding partition at offset o behind j holds for j. From each existing holding partition the live slots come first, at least 1024 and at most 4096 of them; where no holding partition exists all slots are empty; the value 4096 marks an empty slot. Some partition receives 4096 live slots from each of its holding partitions. `face_nbr`: indexes a partition's 4096 cells followed by its lower and then its upper halo cells. A slot that names its own cell stands for no face. On the first and last partition of a group along dom the lower or upper halo cells are ghosts outside the block. `send_map`: [p, 0] are the cells p shares with its lower dom neighbour, [p, 1] those with its upper one, in the order of that neighbour's halo; all 256 of a partition are distinct.
All inputs are finite; a program needn't handle non-finite values.
Results may differ from the reference program's by a relative error of at most 0.000054.
Values sent between devices are 32-bit elements; how exact they have to be, the bound alone decides.
A program may use at most 128 MiB of HBM per device.

```python
import math
import jax
import jax.numpy as jnp
from jax import lax

FIELDS = 8
NF = 12
NB = 7
C_DEV = 4096
PEERS = 32
SLOT = 4096
HALO = 128
N_GROUP = 4
N_DOM = 8


group_steps = (0, 0, 0, 0, 0, 1, -1)


dom_steps = (0, 1, -1, 2, -2, 0, 0)


def draw_ov_source(key, part):
    count_key, owner_key, cell_key = jax.random.split(jax.random.fold_in(key, 11), 3)
    counts = jax.random.randint(count_key, (PEERS, NB), SLOT // 4, SLOT + 1)
    hot_owner = jax.random.randint(owner_key, (), 0, PEERS)
    receiver_ids = jnp.arange(PEERS)[:, None]
    counts = jnp.where(receiver_ids == hot_owner, SLOT, counts)
    group_place = receiver_ids // N_DOM - jnp.array(group_steps)[None, :]
    dom_place = receiver_ids % N_DOM - jnp.array(dom_steps)[None, :]
    holder_real = (group_place >= 0) & (group_place < N_GROUP) & (dom_place >= 0) & (dom_place < N_DOM)
    counts = jnp.where(holder_real, counts, 0)
    cell_ids = jax.random.randint(cell_key, (PEERS, NB, SLOT), 0, C_DEV)
    slot_ids = jnp.arange(SLOT)[None, None, :]
    live = slot_ids < counts[:, :, None]
    return jnp.where(live, cell_ids, C_DEV).astype(jnp.int32)


def draw_face_nbr(key, part):
    kind_key, cell_key = jax.random.split(jax.random.fold_in(key, 23), 2)
    kinds = jax.random.randint(kind_key, (PEERS, NF, C_DEV), 0, 4)
    picks = jax.random.randint(cell_key, (PEERS, NF, C_DEV), 0, C_DEV + 2 * HALO)
    itself = jnp.broadcast_to(jnp.arange(C_DEV, dtype=jnp.int32)[None, None, :], (PEERS, NF, C_DEV))
    return jnp.where(kinds == 0, itself, picks).astype(jnp.int32)


def pick_shared(device_key):
    return jax.random.permutation(device_key, C_DEV)[:2 * HALO]


def draw_send_map(key, part):
    device_keys = jax.random.split(jax.random.fold_in(key, 37), PEERS)
    chosen = jax.vmap(pick_shared)(device_keys)
    return chosen.reshape(PEERS, 2, HALO).astype(jnp.int32)


def touch_ends(entries, own_key, low, largest):
    shape = entries.shape
    place = [jax.random.randint(jax.random.fold_in(own_key, axis), (), 0, shape[axis]) for axis in range(len(shape))]
    entries = entries.at[tuple(place)].set(low)
    longest = shape.index(max(shape))
    place[longest] = (place[longest] + 1) % shape[longest]
    return entries.at[tuple(place)].set(largest)


def block_levels(stream_key, extent, cuts, least, largest):
    def one(position, parts):
        steps = jax.random.uniform(jax.random.fold_in(jax.random.fold_in(stream_key, 6), position), (parts,), jnp.float32, least / len(cuts), largest / len(cuts))
        return jnp.repeat(jnp.exp(steps), extent[position] // parts).reshape((-1,) + (1,) * (len(extent) - position - 1))

    loudness = one(*cuts[0])
    for cut in cuts[1:]:
        loudness = loudness * one(*cut)
    return loudness


def scatter_about(own_key, shape, spread, limit, cuts=(), kind=jnp.bfloat16):
    result = spread * jax.random.normal(own_key, shape, jnp.float32)
    if cuts:
        result = result * block_levels(own_key, shape, cuts, -0.22, 0.18)
    return jnp.clip(result, -limit, limit).astype(kind)


def setup_inputs(seed: int = 0) -> dict:
    seeds = jax.random.split(jax.random.key(seed), 10)
    cotangent = scatter_about(seeds[0], (PEERS, FIELDS, C_DEV), 1.0, 6.0, ((0, 32),), jnp.float32)
    volumes = jnp.clip(jnp.exp(math.log(2.0) - 1.3862944 * jax.random.uniform(seeds[1], (PEERS, C_DEV), jnp.float32) ** block_levels(seeds[1], (PEERS, C_DEV), ((0, 32),), -0.2, 0.2)), 0.5, 2.0)
    ov_target = touch_ends(jax.random.randint(seeds[2], (PEERS, NB, SLOT), 0, C_DEV), jax.random.fold_in(seeds[2], 1), 0, C_DEV - 1).astype(jnp.int32)
    ov_source = draw_ov_source(jax.random.fold_in(seeds[9], 71), 0)
    volume_moment = jnp.clip(jnp.exp(math.log(1.0) - 2.9957323 * jax.random.uniform(seeds[4], (PEERS, NB, SLOT), jnp.float32) ** block_levels(seeds[4], (PEERS, NB, SLOT), ((0, 32),), -0.2, 0.2)), 0.05, 1.0)
    first_moment = scatter_about(seeds[5], (PEERS, 3, NB, SLOT), 0.3, 2.0, ((0, 32),), jnp.float32)
    grad_weight = scatter_about(seeds[6], (PEERS, 3, NF, C_DEV), 0.3, 2.0, ((0, 32),), jnp.float32)
    face_nbr = draw_face_nbr(jax.random.fold_in(seeds[9], 71), 0)
    send_map = draw_send_map(jax.random.fold_in(seeds[9], 71), 0)
    return {"cotangent": cotangent, "volumes": volumes, "ov_target": ov_target, "ov_source": ov_source, "volume_moment": volume_moment, "first_moment": first_moment, "grad_weight": grad_weight, "face_nbr": face_nbr, "send_map": send_map}


group_steps = (0, 0, 0, 0, 0, 1, -1)
dom_steps = (0, 1, -1, 2, -2, 0, 0)


def faces_local(weights, moment_grad, neighbours, halo_width):
    cell_count = weights.shape[2]
    face_terms = jnp.einsum("kfc,kxc->xfc", weights, moment_grad, precision=lax.Precision.HIGHEST)
    field_count = face_terms.shape[0]
    self_part = -jnp.sum(face_terms, axis=1)
    extended = jnp.zeros((field_count, cell_count + 2 * halo_width), face_terms.dtype)
    extended = extended.at[:, neighbours.reshape(-1)].add(face_terms.reshape(field_count, -1))
    return self_part, extended


def move_blocks(values, group_step, dom_step):
    grid = values.reshape((N_GROUP, N_DOM) + values.shape[1:])
    rolled = jnp.roll(grid, (group_step, dom_step), axis=(0, 1))
    group_ids = jnp.arange(N_GROUP, dtype=jnp.int32)[:, None] - group_step
    dom_ids = jnp.arange(N_DOM, dtype=jnp.int32)[None, :] - dom_step
    inside = (group_ids >= 0) & (group_ids < N_GROUP) & (dom_ids >= 0) & (dom_ids < N_DOM)
    inside = inside.reshape((N_GROUP, N_DOM) + (1,) * (values.ndim - 1))
    return jnp.where(inside, rolled, jnp.zeros_like(rolled)).reshape(values.shape)


def scatter_rows(sources, terms):
    empty = jnp.zeros((terms.shape[0], C_DEV + 1), jnp.float32)
    return empty.at[:, sources].add(terms)


def reference(cotangent, volumes, ov_target, ov_source, volume_moment, first_moment, grad_weight, face_nbr, send_map):
    scaled_rows = cotangent / volumes[:, None, :]
    weighted = jax.vmap(lambda rows, targets: rows[:, targets])(scaled_rows, ov_target)
    moments = jnp.concatenate([volume_moment[:, None], first_moment], axis=1)
    summed = jnp.zeros((PEERS, 4 * FIELDS, C_DEV + 1), jnp.float32)
    for offset in range(7):
        terms = (moments[:, :, None, offset] * weighted[:, None, :, offset]).reshape(PEERS, 4 * FIELDS, SLOT)
        arrived = move_blocks(terms, group_steps[offset], dom_steps[offset])
        summed = summed + jax.vmap(scatter_rows)(ov_source[:, offset], arrived)
    moment_sums = summed[..., :C_DEV].reshape(PEERS, 4, FIELDS, C_DEV)

    def per_device(device_data):
        weights, sums_here, neighbours = device_data
        self_part, extended = faces_local(weights, sums_here[1:], neighbours, HALO)
        return sums_here[0] + self_part + extended[:, :C_DEV], extended

    partial_rows, extended = lax.map(per_device, (grad_weight, moment_sums, face_nbr))
    block_grid = extended.reshape(N_GROUP, N_DOM, FIELDS, C_DEV + 2 * HALO)
    upper_blocks = block_grid[..., C_DEV + HALO:]
    lower_blocks = block_grid[..., C_DEV:C_DEV + HALO]
    zero_block = jnp.zeros_like(upper_blocks[:, :1])
    from_lower = jnp.concatenate([zero_block, upper_blocks[:, :-1]], axis=1).reshape(PEERS, FIELDS, HALO)
    from_upper = jnp.concatenate([lower_blocks[:, 1:], zero_block], axis=1).reshape(PEERS, FIELDS, HALO)

    def add_returns(device_data):
        rows_here, lower_rows, upper_rows, shared = device_data
        return rows_here.at[:, shared[0]].add(lower_rows).at[:, shared[1]].add(upper_rows)

    return lax.map(add_returns, (partial_rows, from_lower, from_upper, send_map))
```

```python
import functools
import jax
import jax.numpy as jnp
from jax import lax
from jax.experimental import pallas as pl
from jax.experimental.pallas import tpu as pltpu
from jax.sharding import PartitionSpec as P

LANES = 256
TILE = 128
BF = jnp.bfloat16
F32 = jnp.float32
VMEM = pl.BlockSpec(memory_space=pltpu.VMEM)


def spread(row):
    return jnp.broadcast_to(row, (16, row.shape[1])).astype(F32).astype(BF)


def table_of(low):
    rows = lax.broadcasted_iota(jnp.int32, low.shape, 0).astype(F32).astype(BF)
    one, zero = jnp.ones(low.shape, BF), jnp.zeros(low.shape, BF)
    return jnp.concatenate(
        [jnp.where(low == rows + BF(16 * t), one, zero) for t in range(LANES // 16)], axis=0
    )


def split(value):
    high = value.astype(BF)
    return high, (value - high.astype(F32)).astype(BF)


def masked(tiles, level, count):
    zero = jnp.zeros(level.shape, BF)
    parts = []
    for step in range(count):
        hit = level == BF(step)
        parts.extend(jnp.where(hit, tile, zero) for tile in tiles)
    return jnp.concatenate(parts, axis=0)


def contract(left, right):
    return lax.dot_general(
        left, right, (((1,), (1,)), ((), ())), preferred_element_type=F32
    )


def pick(table, target):
    tiles = table.shape[1] // TILE
    out = []
    for at in range(0, target.shape[1], TILE):
        index = jnp.broadcast_to(target[:, at : at + TILE], (table.shape[0], TILE))
        lane, tile = index & (TILE - 1), index >> 7

        def tree(first, count):
            if count == 1:
                piece = table[:, first * TILE : (first + 1) * TILE]
                return jnp.take_along_axis(piece, lane, axis=1, mode="promise_in_bounds")
            half = 1 << ((count - 1).bit_length() - 1)
            low, high = tree(first, half), tree(first + half, count - half)
            return jnp.where(hits[half], high, low)

        hits = {1 << bit: (tile & (1 << bit)) != 0 for bit in range((tiles - 1).bit_length())}
        out.append(tree(0, tiles))
    return jnp.concatenate(out, axis=1)


def crossing_chunk(table, target, moments, source, levels, total):
    weighted = pick(table, target)
    tops, rests = [], []
    for m in range(4):
        top, rest = split(weighted * moments[m])
        tops.append(top)
        rests.append(rest)
    tiles = [
        jnp.concatenate(pair, axis=0)
        for pair in ((tops[0], tops[1]), (tops[2], tops[3]), (rests[0], rests[1]), (rests[2], rests[3]))
    ]
    left = masked(tiles, spread(source >> 8), levels)
    total[...] += contract(left, table_of(spread(source & (LANES - 1))))


OFFSETS = ((0, 0), (0, 1), (0, -1), (0, 2), (0, -2), (1, 0), (-1, 0))
MESH = pl.DeviceIdType.MESH


def place(shift, count, index):
    there = index + shift
    return there, (there >= 0) & (there < count)


def fused_kernel(
    grid,
    cotangent_far,
    volumes_far,
    targets,
    sources_far,
    volume_moment,
    first_moment,
    weights_far,
    neighbours_far,
    result,
    back,
    cotangent,
    volumes,
    sources,
    weights,
    neighbours,
    table,
    landed_target,
    landed_volume,
    landed_first,
    total,
    sums,
    extended,
    halo,
    send_sem,
    recv_sem,
    halo_send,
    halo_recv,
    early_sem,
    own_sem,
    late_sem,
):
    fields, cells = cotangent.shape
    levels = cells // LANES
    width = halo.shape[2]
    group, dom = lax.axis_index("group"), lax.axis_index("dom")
    def peer(o, sign):
        there_group, group_in = place(sign * OFFSETS[o][0], grid[0], group)
        there_dom, dom_in = place(sign * OFFSETS[o][1], grid[1], dom)
        return (there_group, there_dom), group_in & dom_in

    def copies(o):
        parts = (
            (targets.at[o], landed_target.at[o]),
            (volume_moment.at[o], landed_volume.at[o]),
            (first_moment.at[:, o], landed_first.at[:, o]),
            (table.at[0], table.at[o]),
        )
        return [
            pltpu.make_async_remote_copy(
                src_ref=source,
                dst_ref=to,
                send_sem=send_sem.at[part, o],
                recv_sem=recv_sem.at[part, o],
                device_id=peer(o, 1)[0],
                device_id_type=MESH,
            )
            for part, (source, to) in enumerate(parts)
        ]

    early = [
        pltpu.make_async_copy(source, to, early_sem.at[i])
        for i, (source, to) in enumerate(((cotangent_far.at[0], cotangent), (volumes_far, volumes)))
    ]
    own = [
        pltpu.make_async_copy(source, to, own_sem.at[i])
        for i, (source, to) in enumerate(
            (
                (targets.at[0], landed_target.at[0]),
                (volume_moment.at[0], landed_volume.at[0]),
                (first_moment.at[:, 0], landed_first.at[:, 0]),
                (sources_far, sources),
            )
        )
    ]
    late = [
        pltpu.make_async_copy(weights_far, weights, late_sem.at[0]),
        pltpu.make_async_copy(neighbours_far, neighbours, late_sem.at[1]),
    ]
    for copy in early:
        copy.start()
    barrier = pltpu.get_barrier_semaphore()
    greeted = jnp.int32(0)
    for o in range(1, len(OFFSETS)):
        there, real = peer(o, 1)
        greeted += real.astype(jnp.int32)

        @pl.when(real)
        def _(there=there):
            pl.semaphore_signal(barrier, inc=1, device_id=there, device_id_type=MESH)

    for copy in own + late:
        copy.start()
    total[...] = jnp.zeros_like(total)
    for copy in early:
        copy.wait()
    table[0] = cotangent[...] / volumes[...]
    pl.semaphore_wait(barrier, greeted)

    def send(o):
        @pl.when(peer(o, 1)[1])
        def _():
            for copy in copies(o):
                copy.start()

    send(1)
    send(2)
    for copy in own:
        copy.wait()
    odd = dom % 2

    @pl.loop(0, len(OFFSETS))
    def _(p):
        o = jnp.where(p == 1, 1 + odd, jnp.where(p == 2, 2 - odd, p))
        present = p == 0

        @pl.when(p == 1)
        def _():
            for q in range(3, len(OFFSETS)):
                send(q)

        for q in range(1, len(OFFSETS)):
            real = peer(q, -1)[1] & (o == q)
            present = present | real

            @pl.when(real)
            def _(q=q):
                for copy in copies(q):
                    copy.wait_recv()

        @pl.when(present)
        def _():
            moments = [landed_volume[o]] + [landed_first[m, o] for m in range(3)]
            crossing_chunk(table[o], landed_target[o], moments, sources[o], levels, total)

    for copy in late:
        copy.wait()
    gather_sums(total, sums, result, levels)
    face_pass(sums, extended, weights, neighbours, result, levels + 1)
    for side in range(2):
        cut = slice(side * width, (side + 1) * width)
        halo[side] = both_pieces(extended, 2 * fields * levels, fields, cut)

    lower, has_lower = peer(2, 1)
    upper, has_upper = peer(1, 1)

    def halo_copy(side):
        return pltpu.make_async_remote_copy(
            src_ref=halo.at[side],
            dst_ref=back.at[1 - side],
            send_sem=halo_send.at[side],
            recv_sem=halo_recv.at[1 - side],
            device_id=(lower, upper)[side],
            device_id_type=MESH,
        )

    for side, real in ((0, has_lower), (1, has_upper)):

        @pl.when(real)
        def _(side=side):
            halo_copy(side).start()

        @pl.when(jnp.logical_not(real))
        def _(side=side):
            back[side] = jnp.zeros((fields, width), F32)

    for step in range(levels):
        result[:, step * LANES : (step + 1) * LANES] += both_pieces(extended, 2 * fields * step, fields)

    for o in range(1, len(OFFSETS)):

        @pl.when(peer(o, 1)[1])
        def _(o=o):
            for copy in copies(o):
                copy.wait_send()

    for side, real in ((0, has_lower), (1, has_upper)):

        @pl.when(real)
        def _(side=side):
            halo_copy(side).wait_send()
            halo_copy(1 - side).wait_recv()


def gather_sums(total, sums, result, levels):
    fields = result.shape[0]
    half = 4 * fields
    for step in range(levels):
        at = 2 * half * step
        sums[:, step * LANES : (step + 1) * LANES] = (
            total[at : at + half, :] + total[at + half : at + 2 * half, :]
        )
    result[...] = sums[0:fields, :]


def face_pass(sums, extended, weights, neighbours, result, levels):
    fields = result.shape[0]
    faces = neighbours.shape[0]
    batch = 6 if faces % 6 == 0 else 1
    extended[...] = jnp.zeros_like(extended)

    @pl.loop(0, faces // batch)
    def _(turn):
        lefts, tables, added = [], [], None
        for i in range(batch):
            f = turn * batch + i
            term = sum(weights[k, f] * sums[fields * (k + 1) : fields * (k + 2), :] for k in range(3))
            added = term if added is None else added + term
            cell = neighbours[f]
            lefts.append(masked([jnp.concatenate(split(term), axis=0)], spread(cell >> 8), levels))
            tables.append(table_of(spread(cell & (LANES - 1))))
        extended[...] += contract(jnp.concatenate(lefts, axis=1), jnp.concatenate(tables, axis=1))
        result[...] -= added


def both_pieces(ref, at, fields, cut=slice(None)):
    return ref[at : at + fields, cut] + ref[at + fields : at + 2 * fields, cut]


def return_kernel(result, back, shared, out):
    fields = result.shape[0]
    levels = result.shape[1] // LANES
    top, rest = split(jnp.concatenate([back[0], back[1]], axis=1))
    cell = jnp.concatenate([shared[0], shared[1]], axis=1)
    left = masked([jnp.concatenate([top, rest], axis=0)], spread(cell >> 8), levels)
    added = contract(left, table_of(spread(cell & (LANES - 1))))
    for step in range(levels):
        at = 2 * fields * step
        cut = slice(step * LANES, (step + 1) * LANES)
        out[:, cut] = result[:, cut] + added[at : at + fields] + added[at + fields : at + 2 * fields]


def shards(
    grid,
    cotangent,
    volumes,
    ov_target,
    ov_source,
    volume_moment,
    first_moment,
    grad_weight,
    face_nbr,
    send_map,
):
    fields, cells = cotangent.shape[1:]
    slots = ov_target.shape[2]
    width = send_map.shape[2]
    levels = cells // LANES
    count = len(OFFSETS)
    faces = face_nbr.shape[1]
    far = pl.BlockSpec(memory_space=pl.ANY)
    result, back = pl.pallas_call(
        functools.partial(fused_kernel, grid),
        out_shape=(
            jax.ShapeDtypeStruct((fields, cells), F32),
            jax.ShapeDtypeStruct((2, fields, width), F32),
        ),
        in_specs=[far] * 8,
        out_specs=(VMEM, VMEM),
        scratch_shapes=[
            pltpu.VMEM((fields, cells), F32),
            pltpu.VMEM((1, cells), F32),
            pltpu.VMEM((count, 1, slots), jnp.int32),
            pltpu.VMEM((3, faces, 1, cells), F32),
            pltpu.VMEM((faces, 1, cells), jnp.int32),
            pltpu.VMEM((count, fields, cells), F32),
            pltpu.VMEM((count, 1, slots), jnp.int32),
            pltpu.VMEM((count, 1, slots), F32),
            pltpu.VMEM((3, count, 1, slots), F32),
            pltpu.VMEM((8 * fields * levels, LANES), F32),
            pltpu.VMEM((4 * fields, cells), F32),
            pltpu.VMEM((2 * fields * (levels + 1), LANES), F32),
            pltpu.VMEM((2, fields, width), F32),
            pltpu.SemaphoreType.DMA((4, count)),
            pltpu.SemaphoreType.DMA((4, count)),
            pltpu.SemaphoreType.DMA((2,)),
            pltpu.SemaphoreType.DMA((2,)),
            pltpu.SemaphoreType.DMA((2,)),
            pltpu.SemaphoreType.DMA((4,)),
            pltpu.SemaphoreType.DMA((2,)),
        ],
        compiler_params=pltpu.CompilerParams(
            vmem_limit_bytes=61 * 1024 * 1024, collective_id=0, has_side_effects=True
        ),
    )(
        cotangent,
        volumes,
        jnp.swapaxes(ov_target, 0, 1),
        jnp.swapaxes(ov_source, 0, 1),
        jnp.swapaxes(volume_moment, 0, 1),
        first_moment[0][:, :, None],
        grad_weight[0][:, :, None],
        jnp.swapaxes(face_nbr, 0, 1),
    )
    out = pl.pallas_call(
        return_kernel,
        out_shape=jax.ShapeDtypeStruct((fields, cells), F32),
        in_specs=[VMEM] * 3,
        out_specs=VMEM,
    )(result, back, jnp.swapaxes(send_map, 0, 1))
    return out[None]


def solution(mesh):
    both = ("group", "dom")
    return jax.shard_map(
        functools.partial(shards, (mesh.shape["group"], mesh.shape["dom"])),
        mesh=mesh,
        in_specs=(
            P(both, None, None),
            P(both, None),
            P(both, None, None),
            P(both, None, None),
            P(both, None, None),
            P(both, None, None, None),
            P(both, None, None, None),
            P(both, None, None),
            P(both, None, None),
        ),
        out_specs=P(both, None, None),
        check_vma=False,
    )
```

```python
import functools
import jax
import jax.numpy as jnp
from jax import lax
from jax.experimental import pallas as pl
from jax.experimental.pallas import tpu as pltpu
from jax.sharding import PartitionSpec as P

LANES = 256
TILE = 128
BF = jnp.bfloat16
F32 = jnp.float32
VMEM = pl.BlockSpec(memory_space=pltpu.VMEM)


def spread(row):
    return jnp.broadcast_to(row, (16, row.shape[1])).astype(F32).astype(BF)


def table_of(low):
    rows = lax.broadcasted_iota(jnp.int32, low.shape, 0).astype(F32).astype(BF)
    one, zero = jnp.ones(low.shape, BF), jnp.zeros(low.shape, BF)
    return jnp.concatenate(
        [jnp.where(low == rows + BF(16 * t), one, zero) for t in range(LANES // 16)], axis=0
    )


def split(value):
    high = value.astype(BF)
    return high, (value - high.astype(F32)).astype(BF)


def masked(tiles, level, count):
    zero = jnp.zeros(level.shape, BF)
    parts = []
    for step in range(count):
        hit = level == BF(step)
        parts.extend(jnp.where(hit, tile, zero) for tile in tiles)
    return jnp.concatenate(parts, axis=0)


def contract(left, right):
    return lax.dot_general(
        left, right, (((1,), (1,)), ((), ())), preferred_element_type=F32
    )


def pick(table, target):
    tiles = table.shape[1] // TILE
    out = []
    for at in range(0, target.shape[1], TILE):
        index = jnp.broadcast_to(target[:, at : at + TILE], (table.shape[0], TILE))
        lane, tile = index & (TILE - 1), index >> 7

        def tree(first, count):
            if count == 1:
                piece = table[:, first * TILE : (first + 1) * TILE]
                return jnp.take_along_axis(piece, lane, axis=1, mode="promise_in_bounds")
            half = 1 << ((count - 1).bit_length() - 1)
            low, high = tree(first, half), tree(first + half, count - half)
            return jnp.where(hits[half], high, low)

        hits = {1 << bit: (tile & (1 << bit)) != 0 for bit in range((tiles - 1).bit_length())}
        out.append(tree(0, tiles))
    return jnp.concatenate(out, axis=1)


def halves(weighted, moments):
    pairs = [split(weighted * moment) for moment in moments]
    return [pair[0] for pair in pairs], [pair[1] for pair in pairs]


def slope_tiles(weighted, first):
    top, rest = halves(weighted, first)
    return [jnp.concatenate(pair, axis=0) for pair in ((top[0], top[1]), (top[2], rest[2]), (rest[0], rest[1]))]


def volume_tile(weighted, volume):
    return jnp.concatenate(split(weighted * volume), axis=0)


def level_table(source):
    return spread(source >> 8), table_of(spread(source & (LANES - 1)))


def crossing_chunk(table, target, volume, first, source, levels, slopes, volumes):
    weighted = pick(table, target)
    level, cells = level_table(source)
    left = jnp.concatenate(
        [masked(slope_tiles(weighted, first), level, levels), masked([volume_tile(weighted, volume)], level, levels)],
        axis=0,
    )
    both = contract(left, cells)
    rows = slopes.shape[0]
    slopes[...] += both[:rows]
    volumes[...] += both[rows:]


def slope_chunks(chunks, levels, slopes):
    lefts, tables = [], []
    for table, target, first, source, kept in chunks:
        weighted = pick(table, target)
        kept[...] = weighted
        level, cells = level_table(source)
        lefts.append(masked(slope_tiles(weighted, first), level, levels))
        tables.append(cells)
    slopes[...] += contract(jnp.concatenate(lefts, axis=1), jnp.concatenate(tables, axis=1))


def volume_chunks(chunks, levels, volumes):
    lefts, tables = [], []
    for weighted, volume, source in chunks:
        level, cells = level_table(source)
        lefts.append(masked([volume_tile(weighted, volume)], level, levels))
        tables.append(cells)
    volumes[...] += contract(jnp.concatenate(lefts, axis=1), jnp.concatenate(tables, axis=1))


OFFSETS = ((0, 0), (0, 1), (0, -1), (0, 2), (0, -2), (1, 0), (-1, 0))
FIRST = 3
MESH = pl.DeviceIdType.MESH


def place(shift, count, index):
    there = index + shift
    return there, (there >= 0) & (there < count)


def fused_kernel(
    grid,
    cotangent_far,
    volumes_far,
    targets,
    sources_far,
    volume_moment,
    first_moment,
    weights_far,
    neighbours_far,
    shared_far,
    result,
    back,
    shared,
    cotangent,
    volumes,
    sources,
    weights,
    neighbours,
    table,
    landed_target,
    landed_volume,
    landed_first,
    kept,
    slopes,
    volume_sums,
    sums,
    extended,
    halo,
    nothing,
    send_sem,
    recv_sem,
    halo_send,
    halo_recv,
    early_sem,
    own_sem,
    late_sem,
    fill_sem,
):
    fields, cells = cotangent.shape
    levels = cells // LANES
    width = halo.shape[2]
    group, dom = lax.axis_index("group"), lax.axis_index("dom")
    def peer(o, sign):
        there_group, group_in = place(sign * OFFSETS[o][0], grid[0], group)
        there_dom, dom_in = place(sign * OFFSETS[o][1], grid[1], dom)
        return (there_group, there_dom), group_in & dom_in

    def copies(o):
        parts = (
            (targets.at[o], landed_target.at[o]),
            (volume_moment.at[o], landed_volume.at[o]),
            (first_moment.at[:, o], landed_first.at[:, o]),
            (table.at[0], table.at[o]),
        )
        return [
            pltpu.make_async_remote_copy(
                src_ref=source,
                dst_ref=to,
                send_sem=send_sem.at[part, o],
                recv_sem=recv_sem.at[part, o],
                device_id=peer(o, 1)[0],
                device_id_type=MESH,
            )
            for part, (source, to) in enumerate(parts)
        ]

    early = [
        pltpu.make_async_copy(source, to, early_sem.at[i])
        for i, (source, to) in enumerate(((cotangent_far.at[0], cotangent), (volumes_far, volumes)))
    ]
    own = [
        pltpu.make_async_copy(source, to, own_sem.at[i])
        for i, (source, to) in enumerate(
            (
                (targets.at[0], landed_target.at[0]),
                (volume_moment.at[0], landed_volume.at[0]),
                (first_moment.at[:, 0], landed_first.at[:, 0]),
                (sources_far, sources),
            )
        )
    ]
    late = [
        pltpu.make_async_copy(weights_far, weights, late_sem.at[0]),
        pltpu.make_async_copy(neighbours_far, neighbours, late_sem.at[1]),
        pltpu.make_async_copy(shared_far, shared, late_sem.at[2]),
    ]
    for copy in early:
        copy.start()
    barrier = pltpu.get_barrier_semaphore()
    greeted = jnp.int32(0)
    for o in range(1, len(OFFSETS)):
        there, real = peer(o, 1)
        greeted += real.astype(jnp.int32)

        @pl.when(real)
        def _(there=there):
            pl.semaphore_signal(barrier, inc=1, device_id=there, device_id_type=MESH)

    for copy in own + late:
        copy.start()
    pl.semaphore_wait(barrier, greeted)

    def send(o, parts, wanted=True):
        @pl.when(peer(o, 1)[1] & wanted)
        def _():
            for copy in copies(o)[parts]:
                copy.start()

    odd_group = group % 2
    near = {5: odd_group == 0, 6: odd_group == 1}
    for o in (1, 2):
        send(o, slice(0, 3))
    for o in (5, 6):
        send(o, slice(0, 3), near[o])
    slopes[...] = jnp.zeros_like(slopes)
    volume_sums[...] = jnp.zeros_like(volume_sums)
    nothing[...] = jnp.zeros_like(nothing)
    for copy in early:
        copy.wait()
    table[0] = cotangent[...] / volumes[...]
    for o in (1, 2):
        send(o, slice(3, 4))
    for o in (5, 6):
        send(o, slice(3, 4), near[o])
    for copy in own:
        copy.wait()
    odd = dom % 2

    def arrive(o):
        for q in range(1, len(OFFSETS)):

            @pl.when(peer(q, -1)[1] & (o == q))
            def _(q=q):
                for copy in copies(q):
                    copy.wait_recv()

    def first_moments(o):
        return [landed_first[m, o] for m in range(3)]

    @pl.loop(0, FIRST)
    def _(p):
        o = jnp.where(p == 1, 2 - odd, jnp.where(p == 2, 1 + odd, 0))

        @pl.when(p == 1)
        def _():
            for q in (3, 4):
                send(q, slice(0, 4))
            for q in (5, 6):
                send(q, slice(0, 4), jnp.logical_not(near[q]))

        arrive(o)
        present = p == 0
        for q in (1, 2):
            present = present | (peer(q, -1)[1] & (o == q))

        @pl.when(present)
        def _():
            crossing_chunk(
                table[o], landed_target[o], landed_volume[o], first_moments(o), sources[o], levels, slopes, volume_sums
            )

    @pl.loop(0, (len(OFFSETS) - FIRST) // 2)
    def _(turn):
        pair = [jnp.where(turn == 0, 6 - odd_group, 4), jnp.where(turn == 0, 3, 5 + odd_group)]
        for o in pair:
            arrive(o)
        slope_chunks(
            [(table[o], landed_target[o], first_moments(o), sources[o], kept.at[o - FIRST]) for o in pair],
            levels,
            slopes,
        )

    for copy in late:
        copy.wait()
    gather_sums(slopes, sums, levels)
    result[...] = jnp.zeros_like(result)
    face_pass(sums, extended, weights, neighbours, result, levels + 1)
    for side in range(2):
        cut = slice(side * width, (side + 1) * width)
        halo[side] = both_pieces(extended, 2 * fields * levels, fields, cut)

    lower, has_lower = peer(2, 1)
    upper, has_upper = peer(1, 1)

    def halo_copy(side):
        return pltpu.make_async_remote_copy(
            src_ref=halo.at[side],
            dst_ref=back.at[1 - side],
            send_sem=halo_send.at[side],
            recv_sem=halo_recv.at[1 - side],
            device_id=(lower, upper)[side],
            device_id_type=MESH,
        )

    def fill(side):
        return pltpu.make_async_copy(nothing, back.at[side], fill_sem.at[side])

    for side, real in ((0, has_lower), (1, has_upper)):

        @pl.when(real)
        def _(side=side):
            halo_copy(side).start()

        @pl.when(jnp.logical_not(real))
        def _(side=side):
            fill(side).start()

    volume_chunks(
        [(kept[o - FIRST], landed_volume[o], sources[o]) for o in range(FIRST, len(OFFSETS))], levels, volume_sums
    )
    for step in range(levels):
        at = 2 * fields * step
        result[:, step * LANES : (step + 1) * LANES] += both_pieces(extended, at, fields) + both_pieces(
            volume_sums, at, fields
        )

    for o in range(1, len(OFFSETS)):

        @pl.when(peer(o, 1)[1])
        def _(o=o):
            for copy in copies(o):
                copy.wait_send()

    for side, real in ((0, has_lower), (1, has_upper)):

        @pl.when(real)
        def _(side=side):
            halo_copy(side).wait_send()
            halo_copy(1 - side).wait_recv()

        @pl.when(jnp.logical_not(real))
        def _(side=side):
            fill(side).wait()


def gather_sums(slopes, sums, levels):
    fields = sums.shape[0] // 3
    for step in range(levels):
        x, y, z, low_z, low_x, low_y = (
            slopes[(6 * step + i) * fields : (6 * step + i + 1) * fields, :] for i in range(6)
        )
        sums[:, step * LANES : (step + 1) * LANES] = jnp.concatenate([x + low_x, y + low_y, z + low_z], axis=0)


def face_pass(sums, extended, weights, neighbours, result, levels):
    fields = result.shape[0]
    faces = neighbours.shape[0]
    batch = 6 if faces % 6 == 0 else 1
    extended[...] = jnp.zeros_like(extended)

    @pl.loop(0, faces // batch)
    def _(turn):
        lefts, tables, added = [], [], None
        for i in range(batch):
            f = turn * batch + i
            term = sum(weights[k, f] * sums[fields * k : fields * (k + 1), :] for k in range(3))
            added = term if added is None else added + term
            cell = neighbours[f]
            lefts.append(masked([jnp.concatenate(split(term), axis=0)], spread(cell >> 8), levels))
            tables.append(table_of(spread(cell & (LANES - 1))))
        extended[...] += contract(jnp.concatenate(lefts, axis=1), jnp.concatenate(tables, axis=1))
        result[...] -= added


def both_pieces(ref, at, fields, cut=slice(None)):
    return ref[at : at + fields, cut] + ref[at + fields : at + 2 * fields, cut]


def return_kernel(result, back, shared, out):
    fields = result.shape[0]
    levels = result.shape[1] // LANES
    top, rest = split(jnp.concatenate([back[0], back[1]], axis=1))
    cell = jnp.concatenate([shared[0], shared[1]], axis=1)
    left = masked([jnp.concatenate([top, rest], axis=0)], spread(cell >> 8), levels)
    added = contract(left, table_of(spread(cell & (LANES - 1))))
    for step in range(levels):
        at = 2 * fields * step
        cut = slice(step * LANES, (step + 1) * LANES)
        out[:, cut] = result[:, cut] + added[at : at + fields] + added[at + fields : at + 2 * fields]


def shards(
    grid,
    cotangent,
    volumes,
    ov_target,
    ov_source,
    volume_moment,
    first_moment,
    grad_weight,
    face_nbr,
    send_map,
):
    fields, cells = cotangent.shape[1:]
    slots = ov_target.shape[2]
    width = send_map.shape[2]
    levels = cells // LANES
    count = len(OFFSETS)
    faces = face_nbr.shape[1]
    far = pl.BlockSpec(memory_space=pltpu.HBM)
    result, back, shared = pl.pallas_call(
        functools.partial(fused_kernel, grid),
        out_shape=(
            pltpu.VMEM((fields, cells), F32),
            pltpu.VMEM((2, fields, width), F32),
            pltpu.VMEM((2, 1, width), jnp.int32),
        ),
        in_specs=[far] * 9,
        out_specs=(VMEM, VMEM, VMEM),
        scratch_shapes=[
            pltpu.VMEM((fields, cells), F32),
            pltpu.VMEM((1, cells), F32),
            pltpu.VMEM((count, 1, slots), jnp.int32),
            pltpu.VMEM((3, faces, 1, cells), F32),
            pltpu.VMEM((faces, 1, cells), jnp.int32),
            pltpu.VMEM((count, fields, cells), F32),
            pltpu.VMEM((count, 1, slots), jnp.int32),
            pltpu.VMEM((count, 1, slots), F32),
            pltpu.VMEM((3, count, 1, slots), F32),
            pltpu.VMEM((count - FIRST, fields, slots), F32),
            pltpu.VMEM((6 * fields * levels, LANES), F32),
            pltpu.VMEM((2 * fields * levels, LANES), F32),
            pltpu.VMEM((3 * fields, cells), F32),
            pltpu.VMEM((2 * fields * (levels + 1), LANES), F32),
            pltpu.VMEM((2, fields, width), F32),
            pltpu.VMEM((fields, width), F32),
            pltpu.SemaphoreType.DMA((4, count)),
            pltpu.SemaphoreType.DMA((4, count)),
            pltpu.SemaphoreType.DMA((2,)),
            pltpu.SemaphoreType.DMA((2,)),
            pltpu.SemaphoreType.DMA((2,)),
            pltpu.SemaphoreType.DMA((4,)),
            pltpu.SemaphoreType.DMA((3,)),
            pltpu.SemaphoreType.DMA((2,)),
        ],
        compiler_params=pltpu.CompilerParams(
            vmem_limit_bytes=57 * 1024 * 1024, collective_id=0, has_side_effects=True
        ),
    )(
        cotangent,
        volumes,
        jnp.swapaxes(ov_target, 0, 1),
        jnp.swapaxes(ov_source, 0, 1),
        jnp.swapaxes(volume_moment, 0, 1),
        first_moment[0][:, :, None],
        grad_weight[0][:, :, None],
        jnp.swapaxes(face_nbr, 0, 1),
        jnp.swapaxes(send_map, 0, 1),
    )
    out = pl.pallas_call(
        return_kernel,
        out_shape=jax.ShapeDtypeStruct((fields, cells), F32),
        in_specs=[VMEM] * 3,
        out_specs=VMEM,
        compiler_params=pltpu.CompilerParams(vmem_limit_bytes=4 * 1024 * 1024),
    )(result, back, shared)
    return out[None]


def solution(mesh):
    both = ("group", "dom")
    return jax.shard_map(
        functools.partial(shards, (mesh.shape["group"], mesh.shape["dom"])),
        mesh=mesh,
        in_specs=(
            P(both, None, None),
            P(both, None),
            P(both, None, None),
            P(both, None, None),
            P(both, None, None),
            P(both, None, None, None),
            P(both, None, None, None),
            P(both, None, None),
            P(both, None, None),
        ),
        out_specs=P(both, None, None),
        check_vma=False,
    )
```

```python
import functools
import jax
import jax.numpy as jnp
from jax import lax
from jax.experimental import pallas as pl
from jax.experimental.pallas import tpu as pltpu
from jax.sharding import PartitionSpec as P

LANES = 256
TILE = 128
BF = jnp.bfloat16
F32 = jnp.float32
VMEM = pl.BlockSpec(memory_space=pltpu.VMEM)


def spread(row):
    return jnp.broadcast_to(row, (16, row.shape[1])).astype(F32).astype(BF)


def table_of(low):
    rows = lax.broadcasted_iota(jnp.int32, low.shape, 0).astype(F32).astype(BF)
    one, zero = jnp.ones(low.shape, BF), jnp.zeros(low.shape, BF)
    return jnp.concatenate(
        [jnp.where(low == rows + BF(16 * t), one, zero) for t in range(LANES // 16)], axis=0
    )


def split(value):
    high = value.astype(BF)
    return high, (value - high.astype(F32)).astype(BF)


def masked(tiles, level, count):
    zero = jnp.zeros(level.shape, BF)
    parts = []
    for step in range(count):
        hit = level == BF(step)
        parts.extend(jnp.where(hit, tile, zero) for tile in tiles)
    return jnp.concatenate(parts, axis=0)


def contract(left, right):
    return lax.dot_general(
        left, right, (((1,), (1,)), ((), ())), preferred_element_type=F32
    )


def pick(table, target):
    tiles = table.shape[1] // TILE
    out = []
    for at in range(0, target.shape[1], TILE):
        index = jnp.broadcast_to(target[:, at : at + TILE], (table.shape[0], TILE))
        lane, tile = index & (TILE - 1), index >> 7

        def tree(first, count):
            if count == 1:
                piece = table[:, first * TILE : (first + 1) * TILE]
                return jnp.take_along_axis(piece, lane, axis=1, mode="promise_in_bounds")
            half = 1 << ((count - 1).bit_length() - 1)
            low, high = tree(first, half), tree(first + half, count - half)
            return jnp.where(hits[half], high, low)

        hits = {1 << bit: (tile & (1 << bit)) != 0 for bit in range((tiles - 1).bit_length())}
        out.append(tree(0, tiles))
    return jnp.concatenate(out, axis=1)


def halves(weighted, moments):
    pairs = [split(weighted * moment) for moment in moments]
    return [pair[0] for pair in pairs], [pair[1] for pair in pairs]


def slope_tiles(weighted, first):
    top, rest = halves(weighted, first)
    return [jnp.concatenate(pair, axis=0) for pair in ((top[0], top[1]), (top[2], rest[2]), (rest[0], rest[1]))]


def volume_tile(weighted, volume):
    return jnp.concatenate(split(weighted * volume), axis=0)


def level_table(source):
    return spread(source >> 8), table_of(spread(source & (LANES - 1)))


def crossing_chunk(table, target, volume, first, source, levels, slopes, volumes):
    weighted = pick(table, target)
    level, cells = level_table(source)
    left = jnp.concatenate(
        [masked(slope_tiles(weighted, first), level, levels), masked([volume_tile(weighted, volume)], level, levels)],
        axis=0,
    )
    both = contract(left, cells)
    rows = slopes.shape[0]
    slopes[...] += both[:rows]
    volumes[...] += both[rows:]


def slope_chunks(chunks, levels, slopes):
    lefts, tables = [], []
    for table, target, first, source, kept in chunks:
        weighted = pick(table, target)
        kept[...] = weighted
        level, cells = level_table(source)
        lefts.append(masked(slope_tiles(weighted, first), level, levels))
        tables.append(cells)
    slopes[...] += contract(jnp.concatenate(lefts, axis=1), jnp.concatenate(tables, axis=1))


def volume_chunks(chunks, levels, volumes):
    lefts, tables = [], []
    for weighted, volume, source in chunks:
        level, cells = level_table(source)
        lefts.append(masked([volume_tile(weighted, volume)], level, levels))
        tables.append(cells)
    volumes[...] += contract(jnp.concatenate(lefts, axis=1), jnp.concatenate(tables, axis=1))


OFFSETS = ((0, 0), (0, 1), (0, -1), (0, 2), (0, -2), (1, 0), (-1, 0))
FIRST = 3
MESH = pl.DeviceIdType.MESH


def place(shift, count, index):
    there = index + shift
    return there, (there >= 0) & (there < count)


def fused_kernel(
    grid,
    cotangent_far,
    volumes_far,
    targets,
    sources_far,
    volume_moment,
    first_moment,
    weights_far,
    neighbours_far,
    shared_far,
    result,
    back,
    shared,
    cotangent,
    volumes,
    sources,
    weights,
    neighbours,
    table,
    landed_target,
    landed_volume,
    landed_first,
    kept,
    slopes,
    volume_sums,
    sums,
    extended,
    halo,
    nothing,
    send_sem,
    recv_sem,
    halo_send,
    halo_recv,
    early_sem,
    own_sem,
    late_sem,
    fill_sem,
):
    fields, cells = cotangent.shape
    levels = cells // LANES
    width = halo.shape[2]
    group, dom = lax.axis_index("group"), lax.axis_index("dom")
    def peer(o, sign):
        there_group, group_in = place(sign * OFFSETS[o][0], grid[0], group)
        there_dom, dom_in = place(sign * OFFSETS[o][1], grid[1], dom)
        return (there_group, there_dom), group_in & dom_in

    def copies(o):
        parts = (
            (targets.at[o], landed_target.at[o]),
            (volume_moment.at[o], landed_volume.at[o]),
            (first_moment.at[:, o], landed_first.at[:, o]),
            (table.at[0], table.at[o]),
        )
        return [
            pltpu.make_async_remote_copy(
                src_ref=source,
                dst_ref=to,
                send_sem=send_sem.at[part, o],
                recv_sem=recv_sem.at[part, o],
                device_id=peer(o, 1)[0],
                device_id_type=MESH,
            )
            for part, (source, to) in enumerate(parts)
        ]

    early = [
        pltpu.make_async_copy(source, to, early_sem.at[i])
        for i, (source, to) in enumerate(((cotangent_far.at[0], cotangent), (volumes_far, volumes)))
    ]
    own = [
        pltpu.make_async_copy(source, to, own_sem.at[i])
        for i, (source, to) in enumerate(
            (
                (targets.at[0], landed_target.at[0]),
                (volume_moment.at[0], landed_volume.at[0]),
                (first_moment.at[:, 0], landed_first.at[:, 0]),
                (sources_far, sources),
            )
        )
    ]
    late = [
        pltpu.make_async_copy(weights_far, weights, late_sem.at[0]),
        pltpu.make_async_copy(neighbours_far, neighbours, late_sem.at[1]),
        pltpu.make_async_copy(shared_far, shared, late_sem.at[2]),
    ]
    for copy in early:
        copy.start()
    barrier = pltpu.get_barrier_semaphore()
    greeted = jnp.int32(0)
    for o in range(1, len(OFFSETS)):
        there, real = peer(o, 1)
        greeted += real.astype(jnp.int32)

        @pl.when(real)
        def _(there=there):
            pl.semaphore_signal(barrier, inc=1, device_id=there, device_id_type=MESH)

    for copy in own:
        copy.start()

    def send(o, wanted=True):
        @pl.when(peer(o, 1)[1] & wanted)
        def _():
            for copy in copies(o):
                copy.start()

    odd_group = group % 2
    near = {5: odd_group == 0, 6: odd_group == 1}
    slopes[...] = jnp.zeros_like(slopes)
    volume_sums[...] = jnp.zeros_like(volume_sums)
    nothing[...] = jnp.zeros_like(nothing)
    for copy in early:
        copy.wait()
    table[0] = cotangent[...] / volumes[...]
    for copy in own:
        copy.wait()
    odd = dom % 2

    def arrive(o):
        for q in range(1, len(OFFSETS)):

            @pl.when(peer(q, -1)[1] & (o == q))
            def _(q=q):
                for copy in copies(q):
                    copy.wait_recv()

    def first_moments(o):
        return [landed_first[m, o] for m in range(3)]


    def greet():
        pl.semaphore_wait(barrier, greeted)
        send(2, odd == 0)
        send(1, odd == 1)
        send(1, odd == 0)
        send(2, odd == 1)
        for q in (5, 6):
            send(q, near[q])

    greet()
    for copy in late:
        copy.start()
    crossing_chunk(
        table[0], landed_target[0], landed_volume[0], first_moments(0), sources[0], levels, slopes, volume_sums
    )

    @pl.loop(1, FIRST)
    def _(p):
        o = jnp.where(p == 1, 2 - odd, 1 + odd)

        @pl.when(p == 1)
        def _():
            for q in (3, 4):
                send(q)
            for q in (5, 6):
                send(q, jnp.logical_not(near[q]))

        arrive(o)
        present = peer(1, -1)[1] & (o == 1) | peer(2, -1)[1] & (o == 2)

        @pl.when(present)
        def _():
            crossing_chunk(
                table[o], landed_target[o], landed_volume[o], first_moments(o), sources[o], levels, slopes, volume_sums
            )

    last = jnp.where(odd_group == 1, peer(6, -1)[1], peer(5, -1)[1])

    def chunk(o):
        return table[o], landed_target[o], first_moments(o), sources[o], kept.at[o - FIRST]

    @pl.loop(0, 3)
    def _(turn):
        @pl.when(turn == 1)
        def _():
            for o in (3, 4):
                arrive(o)
            slope_chunks([chunk(o) for o in (3, 4)], levels, slopes)

        o = jnp.where(turn == 0, 6 - odd_group, 5 + odd_group)

        @pl.when((turn == 0) | ((turn == 2) & last))
        def _():
            arrive(o)
            slope_chunks([chunk(o)], levels, slopes)

        @pl.when((turn == 2) & jnp.logical_not(last))
        def _():
            kept[o - FIRST] = jnp.zeros_like(cotangent)

    for copy in late:
        copy.wait()
    gather_sums(slopes, sums, levels)
    result[...] = jnp.zeros_like(result)
    face_pass(sums, extended, weights, neighbours, result, levels + 1)
    for side in range(2):
        cut = slice(side * width, (side + 1) * width)
        halo[side] = both_pieces(extended, 2 * fields * levels, fields, cut)

    lower, has_lower = peer(2, 1)
    upper, has_upper = peer(1, 1)

    def halo_copy(side):
        return pltpu.make_async_remote_copy(
            src_ref=halo.at[side],
            dst_ref=back.at[1 - side],
            send_sem=halo_send.at[side],
            recv_sem=halo_recv.at[1 - side],
            device_id=(lower, upper)[side],
            device_id_type=MESH,
        )

    def fill(side):
        return pltpu.make_async_copy(nothing, back.at[side], fill_sem.at[side])

    for side, real in ((0, has_lower), (1, has_upper)):

        @pl.when(real)
        def _(side=side):
            halo_copy(side).start()

        @pl.when(jnp.logical_not(real))
        def _(side=side):
            fill(side).start()

    volume_chunks(
        [(kept[o - FIRST], landed_volume[o], sources[o]) for o in range(FIRST, len(OFFSETS))],
        levels,
        volume_sums,
    )
    for step in range(levels):
        at = 2 * fields * step
        result[:, step * LANES : (step + 1) * LANES] += both_pieces(extended, at, fields) + both_pieces(
            volume_sums, at, fields
        )

    for o in range(1, len(OFFSETS)):

        @pl.when(peer(o, 1)[1])
        def _(o=o):
            for copy in copies(o):
                copy.wait_send()

    for side, real in ((0, has_lower), (1, has_upper)):

        @pl.when(real)
        def _(side=side):
            halo_copy(side).wait_send()
            halo_copy(1 - side).wait_recv()

        @pl.when(jnp.logical_not(real))
        def _(side=side):
            fill(side).wait()


def gather_sums(slopes, sums, levels):
    fields = sums.shape[0] // 3
    for step in range(levels):
        x, y, z, low_z, low_x, low_y = (
            slopes[(6 * step + i) * fields : (6 * step + i + 1) * fields, :] for i in range(6)
        )
        sums[:, step * LANES : (step + 1) * LANES] = jnp.concatenate([x + low_x, y + low_y, z + low_z], axis=0)


def face_pass(sums, extended, weights, neighbours, result, levels):
    fields = result.shape[0]
    faces = neighbours.shape[0]
    batch = 6 if faces % 6 == 0 else 1
    extended[...] = jnp.zeros_like(extended)

    @pl.loop(0, faces // batch)
    def _(turn):
        lefts, tables, added = [], [], None
        for i in range(batch):
            f = turn * batch + i
            term = sum(weights[k, f] * sums[fields * k : fields * (k + 1), :] for k in range(3))
            added = term if added is None else added + term
            cell = neighbours[f]
            lefts.append(masked([jnp.concatenate(split(term), axis=0)], spread(cell >> 8), levels))
            tables.append(table_of(spread(cell & (LANES - 1))))
        extended[...] += contract(jnp.concatenate(lefts, axis=1), jnp.concatenate(tables, axis=1))
        result[...] -= added


def both_pieces(ref, at, fields, cut=slice(None)):
    return ref[at : at + fields, cut] + ref[at + fields : at + 2 * fields, cut]


def return_kernel(result, back, shared, out):
    fields = result.shape[0]
    levels = result.shape[1] // LANES
    top, rest = split(jnp.concatenate([back[0], back[1]], axis=1))
    cell = jnp.concatenate([shared[0], shared[1]], axis=1)
    left = masked([jnp.concatenate([top, rest], axis=0)], spread(cell >> 8), levels)
    added = contract(left, table_of(spread(cell & (LANES - 1))))
    for step in range(levels):
        at = 2 * fields * step
        cut = slice(step * LANES, (step + 1) * LANES)
        out[:, cut] = result[:, cut] + added[at : at + fields] + added[at + fields : at + 2 * fields]


def shards(
    grid,
    cotangent,
    volumes,
    ov_target,
    ov_source,
    volume_moment,
    first_moment,
    grad_weight,
    face_nbr,
    send_map,
):
    fields, cells = cotangent.shape[1:]
    slots = ov_target.shape[2]
    width = send_map.shape[2]
    levels = cells // LANES
    count = len(OFFSETS)
    faces = face_nbr.shape[1]
    far = pl.BlockSpec(memory_space=pltpu.HBM)
    result, back, shared = pl.pallas_call(
        functools.partial(fused_kernel, grid),
        out_shape=(
            pltpu.VMEM((fields, cells), F32),
            pltpu.VMEM((2, fields, width), F32),
            pltpu.VMEM((2, 1, width), jnp.int32),
        ),
        in_specs=[far] * 9,
        out_specs=(VMEM, VMEM, VMEM),
        scratch_shapes=[
            pltpu.VMEM((fields, cells), F32),
            pltpu.VMEM((1, cells), F32),
            pltpu.VMEM((count, 1, slots), jnp.int32),
            pltpu.VMEM((3, faces, 1, cells), F32),
            pltpu.VMEM((faces, 1, cells), jnp.int32),
            pltpu.VMEM((count, fields, cells), F32),
            pltpu.VMEM((count, 1, slots), jnp.int32),
            pltpu.VMEM((count, 1, slots), F32),
            pltpu.VMEM((3, count, 1, slots), F32),
            pltpu.VMEM((count - FIRST, fields, slots), F32),
            pltpu.VMEM((6 * fields * levels, LANES), F32),
            pltpu.VMEM((2 * fields * levels, LANES), F32),
            pltpu.VMEM((3 * fields, cells), F32),
            pltpu.VMEM((2 * fields * (levels + 1), LANES), F32),
            pltpu.VMEM((2, fields, width), F32),
            pltpu.VMEM((fields, width), F32),
            pltpu.SemaphoreType.DMA((4, count)),
            pltpu.SemaphoreType.DMA((4, count)),
            pltpu.SemaphoreType.DMA((2,)),
            pltpu.SemaphoreType.DMA((2,)),
            pltpu.SemaphoreType.DMA((2,)),
            pltpu.SemaphoreType.DMA((4,)),
            pltpu.SemaphoreType.DMA((3,)),
            pltpu.SemaphoreType.DMA((2,)),
        ],
        compiler_params=pltpu.CompilerParams(
            vmem_limit_bytes=57 * 1024 * 1024, collective_id=0, has_side_effects=True
        ),
    )(
        cotangent,
        volumes,
        jnp.swapaxes(ov_target, 0, 1),
        jnp.swapaxes(ov_source, 0, 1),
        jnp.swapaxes(volume_moment, 0, 1),
        first_moment[0][:, :, None],
        grad_weight[0][:, :, None],
        jnp.swapaxes(face_nbr, 0, 1),
        jnp.swapaxes(send_map, 0, 1),
    )
    out = pl.pallas_call(
        return_kernel,
        out_shape=jax.ShapeDtypeStruct((fields, cells), F32),
        in_specs=[VMEM] * 3,
        out_specs=VMEM,
        compiler_params=pltpu.CompilerParams(vmem_limit_bytes=4 * 1024 * 1024),
    )(result, back, shared)
    return out[None]


def solution(mesh):
    both = ("group", "dom")
    return jax.shard_map(
        functools.partial(shards, (mesh.shape["group"], mesh.shape["dom"])),
        mesh=mesh,
        in_specs=(
            P(both, None, None),
            P(both, None),
            P(both, None, None),
            P(both, None, None),
            P(both, None, None),
            P(both, None, None, None),
            P(both, None, None, None),
            P(both, None, None),
            P(both, None, None),
        ),
        out_specs=P(both, None, None),
        check_vma=False,
    )
```

```python
import functools
import jax
import jax.numpy as jnp
from jax import lax
from jax.experimental import pallas as pl
from jax.experimental.pallas import tpu as pltpu
from jax.sharding import PartitionSpec as P

LANES = 256
TILE = 128
BF = jnp.bfloat16
F32 = jnp.float32
VMEM = pl.BlockSpec(memory_space=pltpu.VMEM)


def spread(row):
    return jnp.broadcast_to(row, (16, row.shape[1])).astype(F32).astype(BF)


def table_of(low):
    rows = lax.broadcasted_iota(jnp.int32, low.shape, 0).astype(F32).astype(BF)
    one, zero = jnp.ones(low.shape, BF), jnp.zeros(low.shape, BF)
    return jnp.concatenate(
        [jnp.where(low == rows + BF(16 * t), one, zero) for t in range(LANES // 16)], axis=0
    )


def split(value):
    high = value.astype(BF)
    return high, (value - high.astype(F32)).astype(BF)


def masked(tiles, level, count):
    zero = jnp.zeros(level.shape, BF)
    parts = []
    for step in range(count):
        hit = level == BF(step)
        parts.extend(jnp.where(hit, tile, zero) for tile in tiles)
    return jnp.concatenate(parts, axis=0)


def contract(left, right):
    return lax.dot_general(
        left, right, (((1,), (1,)), ((), ())), preferred_element_type=F32
    )


def pick(table, target):
    tiles = table.shape[1] // TILE
    out = []
    for at in range(0, target.shape[1], TILE):
        index = jnp.broadcast_to(target[:, at : at + TILE], (table.shape[0], TILE))
        lane, tile = index & (TILE - 1), index >> 7

        def tree(first, count):
            if count == 1:
                piece = table[:, first * TILE : (first + 1) * TILE]
                return jnp.take_along_axis(piece, lane, axis=1, mode="promise_in_bounds")
            half = 1 << ((count - 1).bit_length() - 1)
            low, high = tree(first, half), tree(first + half, count - half)
            return jnp.where(hits[half], high, low)

        hits = {1 << bit: (tile & (1 << bit)) != 0 for bit in range((tiles - 1).bit_length())}
        out.append(tree(0, tiles))
    return jnp.concatenate(out, axis=1)


def halves(weighted, moments):
    pairs = [split(weighted * moment) for moment in moments]
    return [pair[0] for pair in pairs], [pair[1] for pair in pairs]


def slope_tiles(weighted, first):
    top, rest = halves(weighted, first)
    return [jnp.concatenate(pair, axis=0) for pair in ((top[0], top[1]), (top[2], rest[2]), (rest[0], rest[1]))]


def volume_tile(weighted, volume):
    return jnp.concatenate(split(weighted * volume), axis=0)


def level_table(source):
    return spread(source >> 8), table_of(spread(source & (LANES - 1)))


def crossing_chunk(table, target, volume, first, source, levels, slopes, volumes):
    weighted = pick(table, target)
    level, cells = level_table(source)
    left = jnp.concatenate(
        [masked(slope_tiles(weighted, first), level, levels), masked([volume_tile(weighted, volume)], level, levels)],
        axis=0,
    )
    both = contract(left, cells)
    rows = slopes.shape[0]
    slopes[...] += both[:rows]
    volumes[...] += both[rows:]


def slope_chunks(chunks, levels, slopes):
    lefts, tables = [], []
    for table, target, first, source, kept in chunks:
        weighted = pick(table, target)
        kept[...] = weighted
        level, cells = level_table(source)
        lefts.append(masked(slope_tiles(weighted, first), level, levels))
        tables.append(cells)
    slopes[...] += contract(jnp.concatenate(lefts, axis=1), jnp.concatenate(tables, axis=1))


def volume_chunks(chunks, levels, volumes):
    lefts, tables = [], []
    for weighted, volume, source in chunks:
        level, cells = level_table(source)
        lefts.append(masked([volume_tile(weighted, volume)], level, levels))
        tables.append(cells)
    volumes[...] += contract(jnp.concatenate(lefts, axis=1), jnp.concatenate(tables, axis=1))


OFFSETS = ((0, 0), (0, 1), (0, -1), (0, 2), (0, -2), (1, 0), (-1, 0))
FIRST = 3
MESH = pl.DeviceIdType.MESH


def place(shift, count, index):
    there = index + shift
    return there, (there >= 0) & (there < count)


def fused_kernel(
    grid,
    cotangent_far,
    volumes_far,
    targets,
    sources_far,
    volume_moment,
    first_moment,
    weights_far,
    neighbours_far,
    shared_far,
    result,
    back,
    shared,
    cotangent,
    volumes,
    sources,
    weights,
    neighbours,
    table,
    landed_target,
    landed_volume,
    landed_first,
    kept,
    slopes,
    volume_sums,
    sums,
    extended,
    halo,
    nothing,
    send_sem,
    recv_sem,
    halo_send,
    halo_recv,
    early_sem,
    own_sem,
    late_sem,
    fill_sem,
):
    fields, cells = cotangent.shape
    levels = cells // LANES
    width = halo.shape[2]
    group, dom = lax.axis_index("group"), lax.axis_index("dom")
    def peer(o, sign):
        there_group, group_in = place(sign * OFFSETS[o][0], grid[0], group)
        there_dom, dom_in = place(sign * OFFSETS[o][1], grid[1], dom)
        return (there_group, there_dom), group_in & dom_in

    def copies(o):
        parts = (
            (targets.at[o], landed_target.at[o]),
            (volume_moment.at[o], landed_volume.at[o]),
            (first_moment.at[:, o], landed_first.at[:, o]),
            (table.at[0], table.at[o]),
        )
        return [
            pltpu.make_async_remote_copy(
                src_ref=source,
                dst_ref=to,
                send_sem=send_sem.at[part, o],
                recv_sem=recv_sem.at[part, o],
                device_id=peer(o, 1)[0],
                device_id_type=MESH,
            )
            for part, (source, to) in enumerate(parts)
        ]

    early = [
        pltpu.make_async_copy(source, to, early_sem.at[i])
        for i, (source, to) in enumerate(((cotangent_far.at[0], cotangent), (volumes_far, volumes)))
    ]
    own = [
        pltpu.make_async_copy(source, to, own_sem.at[i])
        for i, (source, to) in enumerate(
            (
                (targets.at[0], landed_target.at[0]),
                (volume_moment.at[0], landed_volume.at[0]),
                (first_moment.at[:, 0], landed_first.at[:, 0]),
                (sources_far, sources),
            )
        )
    ]
    late = [
        pltpu.make_async_copy(weights_far, weights, late_sem.at[0]),
        pltpu.make_async_copy(neighbours_far, neighbours, late_sem.at[1]),
        pltpu.make_async_copy(shared_far, shared, late_sem.at[2]),
    ]
    for copy in early:
        copy.start()
    barrier = pltpu.get_barrier_semaphore()
    greeted = jnp.int32(0)
    for o in range(1, len(OFFSETS)):
        there, real = peer(o, 1)
        greeted += real.astype(jnp.int32)

        @pl.when(real)
        def _(there=there):
            pl.semaphore_signal(barrier, inc=1, device_id=there, device_id_type=MESH)

    for copy in own:
        copy.start()

    def send(o, wanted=True):
        @pl.when(peer(o, 1)[1] & wanted)
        def _():
            for copy in copies(o):
                copy.start()

    odd_group = group % 2
    near = {5: odd_group == 0, 6: odd_group == 1}
    slopes[...] = jnp.zeros_like(slopes)
    volume_sums[...] = jnp.zeros_like(volume_sums)
    nothing[...] = jnp.zeros_like(nothing)
    for copy in early:
        copy.wait()
    table[0] = cotangent[...] / volumes[...]
    for copy in own:
        copy.wait()
    odd = dom % 2

    def arrive(o):
        for q in range(1, len(OFFSETS)):

            @pl.when(peer(q, -1)[1] & (o == q))
            def _(q=q):
                for copy in copies(q):
                    copy.wait_recv()

    def first_moments(o):
        return [landed_first[m, o] for m in range(3)]


    def greet():
        pl.semaphore_wait(barrier, greeted)
        send(1, odd == 0)
        send(2, odd == 1)
        send(2, odd == 0)
        send(1, odd == 1)
        for q in (5, 6):
            send(q, near[q])

    greet()
    for copy in late:
        copy.start()
    crossing_chunk(
        table[0], landed_target[0], landed_volume[0], first_moments(0), sources[0], levels, slopes, volume_sums
    )

    @pl.loop(1, FIRST)
    def _(p):
        o = jnp.where(p == 1, 2 - odd, 1 + odd)

        @pl.when(p == 1)
        def _():
            for q in (3, 4):
                send(q)

        @pl.when(p == 2)
        def _():
            for q in (5, 6):
                send(q, jnp.logical_not(near[q]))

        arrive(o)
        present = peer(1, -1)[1] & (o == 1) | peer(2, -1)[1] & (o == 2)

        @pl.when(present)
        def _():
            crossing_chunk(
                table[o], landed_target[o], landed_volume[o], first_moments(o), sources[o], levels, slopes, volume_sums
            )

    last = jnp.where(odd_group == 1, peer(6, -1)[1], peer(5, -1)[1])

    def chunk(o):
        return table[o], landed_target[o], first_moments(o), sources[o], kept.at[o - FIRST]

    @pl.loop(0, 3)
    def _(turn):
        @pl.when(turn == 1)
        def _():
            for o in (3, 4):
                arrive(o)
            slope_chunks([chunk(o) for o in (3, 4)], levels, slopes)

        o = jnp.where(turn == 0, 6 - odd_group, 5 + odd_group)

        @pl.when((turn == 0) | ((turn == 2) & last))
        def _():
            arrive(o)
            slope_chunks([chunk(o)], levels, slopes)

        @pl.when((turn == 2) & jnp.logical_not(last))
        def _():
            kept[o - FIRST] = jnp.zeros_like(cotangent)

    for copy in late:
        copy.wait()
    gather_sums(slopes, sums, levels)
    result[...] = jnp.zeros_like(result)
    face_pass(sums, extended, weights, neighbours, result, levels + 1)
    for side in range(2):
        cut = slice(side * width, (side + 1) * width)
        halo[side] = both_pieces(extended, 2 * fields * levels, fields, cut)

    lower, has_lower = peer(2, 1)
    upper, has_upper = peer(1, 1)

    def halo_copy(side):
        return pltpu.make_async_remote_copy(
            src_ref=halo.at[side],
            dst_ref=back.at[1 - side],
            send_sem=halo_send.at[side],
            recv_sem=halo_recv.at[1 - side],
            device_id=(lower, upper)[side],
            device_id_type=MESH,
        )

    def fill(side):
        return pltpu.make_async_copy(nothing, back.at[side], fill_sem.at[side])

    for side, real in ((0, has_lower), (1, has_upper)):

        @pl.when(real)
        def _(side=side):
            halo_copy(side).start()

        @pl.when(jnp.logical_not(real))
        def _(side=side):
            fill(side).start()

    volume_chunks(
        [(kept[o - FIRST], landed_volume[o], sources[o]) for o in range(FIRST, len(OFFSETS))],
        levels,
        volume_sums,
    )
    for step in range(levels):
        at = 2 * fields * step
        result[:, step * LANES : (step + 1) * LANES] += both_pieces(extended, at, fields) + both_pieces(
            volume_sums, at, fields
        )

    for o in range(1, len(OFFSETS)):

        @pl.when(peer(o, 1)[1])
        def _(o=o):
            for copy in copies(o):
                copy.wait_send()

    for side, real in ((0, has_lower), (1, has_upper)):

        @pl.when(real)
        def _(side=side):
            halo_copy(side).wait_send()
            halo_copy(1 - side).wait_recv()

        @pl.when(jnp.logical_not(real))
        def _(side=side):
            fill(side).wait()


def gather_sums(slopes, sums, levels):
    fields = sums.shape[0] // 3
    for step in range(levels):
        x, y, z, low_z, low_x, low_y = (
            slopes[(6 * step + i) * fields : (6 * step + i + 1) * fields, :] for i in range(6)
        )
        sums[:, step * LANES : (step + 1) * LANES] = jnp.concatenate([x + low_x, y + low_y, z + low_z], axis=0)


def face_pass(sums, extended, weights, neighbours, result, levels):
    fields = result.shape[0]
    faces = neighbours.shape[0]
    batch = 6 if faces % 6 == 0 else 1
    extended[...] = jnp.zeros_like(extended)

    @pl.loop(0, faces // batch)
    def _(turn):
        lefts, tables, added = [], [], None
        for i in range(batch):
            f = turn * batch + i
            term = sum(weights[k, f] * sums[fields * k : fields * (k + 1), :] for k in range(3))
            added = term if added is None else added + term
            cell = neighbours[f]
            lefts.append(masked([jnp.concatenate(split(term), axis=0)], spread(cell >> 8), levels))
            tables.append(table_of(spread(cell & (LANES - 1))))
        extended[...] += contract(jnp.concatenate(lefts, axis=1), jnp.concatenate(tables, axis=1))
        result[...] -= added


def both_pieces(ref, at, fields, cut=slice(None)):
    return ref[at : at + fields, cut] + ref[at + fields : at + 2 * fields, cut]


def return_kernel(result, back, shared, out):
    fields = result.shape[0]
    levels = result.shape[1] // LANES
    top, rest = split(jnp.concatenate([back[0], back[1]], axis=1))
    cell = jnp.concatenate([shared[0], shared[1]], axis=1)
    left = masked([jnp.concatenate([top, rest], axis=0)], spread(cell >> 8), levels)
    added = contract(left, table_of(spread(cell & (LANES - 1))))
    for step in range(levels):
        at = 2 * fields * step
        cut = slice(step * LANES, (step + 1) * LANES)
        out[:, cut] = result[:, cut] + added[at : at + fields] + added[at + fields : at + 2 * fields]


def shards(
    grid,
    cotangent,
    volumes,
    ov_target,
    ov_source,
    volume_moment,
    first_moment,
    grad_weight,
    face_nbr,
    send_map,
):
    fields, cells = cotangent.shape[1:]
    slots = ov_target.shape[2]
    width = send_map.shape[2]
    levels = cells // LANES
    count = len(OFFSETS)
    faces = face_nbr.shape[1]
    far = pl.BlockSpec(memory_space=pltpu.HBM)
    result, back, shared = pl.pallas_call(
        functools.partial(fused_kernel, grid),
        out_shape=(
            pltpu.VMEM((fields, cells), F32),
            pltpu.VMEM((2, fields, width), F32),
            pltpu.VMEM((2, 1, width), jnp.int32),
        ),
        in_specs=[far] * 9,
        out_specs=(VMEM, VMEM, VMEM),
        scratch_shapes=[
            pltpu.VMEM((fields, cells), F32),
            pltpu.VMEM((1, cells), F32),
            pltpu.VMEM((count, 1, slots), jnp.int32),
            pltpu.VMEM((3, faces, 1, cells), F32),
            pltpu.VMEM((faces, 1, cells), jnp.int32),
            pltpu.VMEM((count, fields, cells), F32),
            pltpu.VMEM((count, 1, slots), jnp.int32),
            pltpu.VMEM((count, 1, slots), F32),
            pltpu.VMEM((3, count, 1, slots), F32),
            pltpu.VMEM((count - FIRST, fields, slots), F32),
            pltpu.VMEM((6 * fields * levels, LANES), F32),
            pltpu.VMEM((2 * fields * levels, LANES), F32),
            pltpu.VMEM((3 * fields, cells), F32),
            pltpu.VMEM((2 * fields * (levels + 1), LANES), F32),
            pltpu.VMEM((2, fields, width), F32),
            pltpu.VMEM((fields, width), F32),
            pltpu.SemaphoreType.DMA((4, count)),
            pltpu.SemaphoreType.DMA((4, count)),
            pltpu.SemaphoreType.DMA((2,)),
            pltpu.SemaphoreType.DMA((2,)),
            pltpu.SemaphoreType.DMA((2,)),
            pltpu.SemaphoreType.DMA((4,)),
            pltpu.SemaphoreType.DMA((3,)),
            pltpu.SemaphoreType.DMA((2,)),
        ],
        compiler_params=pltpu.CompilerParams(
            vmem_limit_bytes=57 * 1024 * 1024, collective_id=0, has_side_effects=True
        ),
    )(
        cotangent,
        volumes,
        jnp.swapaxes(ov_target, 0, 1),
        jnp.swapaxes(ov_source, 0, 1),
        jnp.swapaxes(volume_moment, 0, 1),
        first_moment[0][:, :, None],
        grad_weight[0][:, :, None],
        jnp.swapaxes(face_nbr, 0, 1),
        jnp.swapaxes(send_map, 0, 1),
    )
    out = pl.pallas_call(
        return_kernel,
        out_shape=jax.ShapeDtypeStruct((fields, cells), F32),
        in_specs=[VMEM] * 3,
        out_specs=VMEM,
        compiler_params=pltpu.CompilerParams(vmem_limit_bytes=4 * 1024 * 1024),
    )(result, back, shared)
    return out[None]


def solution(mesh):
    both = ("group", "dom")
    return jax.shard_map(
        functools.partial(shards, (mesh.shape["group"], mesh.shape["dom"])),
        mesh=mesh,
        in_specs=(
            P(both, None, None),
            P(both, None),
            P(both, None, None),
            P(both, None, None),
            P(both, None, None),
            P(both, None, None, None),
            P(both, None, None, None),
            P(both, None, None),
            P(both, None, None),
        ),
        out_specs=P(both, None, None),
        check_vma=False,
    )
```
